512 devices in a mesh: blk: 8 (over x, core), team: 64 (over y, z).
Axes of the slice: x: 4, y: 4, z: 16, core: 2. Of those that a mesh axis runs over, the one named last changes fastest.
Arguments:
- queries: bfloat16 [8, 1024, 512], P('blk', 'team'), may hold values from -6 to 6
- keys: bfloat16 [8, 64, 256, 512], P('blk', 'team'), may hold values from -6 to 6
- values: bfloat16 [8, 64, 256, 512], P('blk', 'team'), may hold values from -40 to 40
- block_ids: int32 [8, 64, 8, 8], P('blk', 'team'), may hold values from 0 to 15, as said below
- masks: int32 [8, 64, 8, 8, 16, 128], P('blk', 'team'), may hold values from 0 to 255
- gate_input: bfloat16 [8, 1024, 512], P('blk', 'team'), may hold values from -6 to 6
- w_gate: bfloat16 [512, 512], replicated, may hold values from -0.25 to 0.25
Outputs:
- gated: bfloat16 [8, 1024, 512], P('blk', 'team')
The draws below stay inside these ranges and needn't reach their ends.
Inputs may be any that keep to these rules, and one draw needn't show every extreme that they name: `block_ids`: each query tile lists 8 distinct blocks of its team; block c is 128 rows starting at (c % 2) * 128 of the key owner c // 2 along blk in the same team. Bit i of masks[g, t, q, j, w, a] is the mask between query row a of tile q and key row 8 w + i of listed block j.
All inputs are finite; a program needn't handle non-finite values.
Results may differ from the reference program's by a relative error of at most 0.0049.
Values may be sent and summed in bfloat16 or wider, within the bound.
No kernel may reach another device: no remote copies, remote signals or barrier semaphores. Data moves between devices by JAX's collectives and lax.ppermute only.
A program may use at most 64 MiB of HBM per device.

```python
import math
import jax
import jax.numpy as jnp
from jax import lax

F = 512
TILE = 128
QT = 8
KB = 2
NB = 8
QG = 1024
KV_DEV = 256
WORDS = 16
N_BLK = 8
N_TEAM = 64


def draw_block_ids(key, part):
    lists = N_BLK * N_TEAM * QT
    list_keys = jax.random.split(key, lists)

    def draw_list(list_key):
        return jax.random.permutation(list_key, N_BLK * KB)[:NB].astype(jnp.int32)
    return jax.vmap(draw_list)(list_keys).reshape(N_BLK, N_TEAM, QT, NB)


def draw_values(key, part):
    key_cols, key_base = jax.random.split(key, 2)
    full_shape = (N_BLK, N_TEAM, KV_DEV, F)
    col_scale = jnp.exp(jax.random.uniform(key_cols, (F,), jnp.float32) * math.log(10.0))
    base_draw = jnp.clip(jax.random.normal(key_base, full_shape, jnp.float32), -4.0, 4.0)
    return (base_draw * col_scale).astype(jnp.bfloat16)


def with_ends(result, rng, low, largest):
    spot = [jax.random.randint(jax.random.fold_in(rng, axis), (), 0, length) for axis, length in enumerate(result.shape)]
    widest = result.shape.index(max(result.shape))
    next_to = spot[:widest] + [(spot[widest] + 1) % result.shape[widest]] + spot[widest + 1:]
    return result.at[tuple(spot)].set(low).at[tuple(next_to)].set(largest)


def steps_of(own_key, extent, cuts, low, largest):
    gain, own = 1.0, jax.random.fold_in(own_key, 6)
    for axis_at, blocks in cuts:
        draws = jnp.exp(jax.random.uniform(jax.random.fold_in(own, axis_at), (blocks,), jnp.float32, low / len(cuts), largest / len(cuts)))
        gain = gain * jnp.repeat(draws, extent[axis_at] // blocks).reshape([-1 if axis == axis_at else 1 for axis in range(len(extent))])
    return gain


def scatter_about(stream_key, shape, deviation, limit, shards=(), held_as=jnp.bfloat16):
    values = jax.random.normal(stream_key, shape, jnp.float32) * deviation
    if len(shards) > 0:
        values = steps_of(stream_key, shape, shards, -0.22, 0.18) * values
    return jnp.clip(values, min=-limit, max=limit).astype(held_as)


def setup_inputs(seed: int = 0) -> dict:
    key_list = jax.random.split(jax.random.key(seed), 8)
    queries = scatter_about(key_list[0], (N_BLK, QG, F), 1.0, 6.0, ((0, 8), (1, 64)))
    keys = scatter_about(key_list[1], (N_BLK, N_TEAM, KV_DEV, F), 1.0, 6.0, ((0, 8), (1, 64)))
    values = draw_values(jax.random.fold_in(key_list[7], 71), 0)
    block_ids = draw_block_ids(jax.random.fold_in(key_list[7], 71), 0)
    masks = with_ends(jax.random.randint(key_list[4], (N_BLK, N_TEAM, QT, NB, WORDS, TILE), 0, 256), jax.random.fold_in(key_list[4], 1), 0, 255).astype(jnp.int32)
    gate_input = scatter_about(key_list[5], (N_BLK, QG, F), 1.0, 6.0, ((0, 8), (1, 64)))
    w_gate = scatter_about(key_list[6], (F, F), F ** -0.5, 0.25)
    return dict(queries=queries, keys=keys, values=values, block_ids=block_ids, masks=masks, gate_input=gate_input, w_gate=w_gate)


def unpack(packed):
    shifts = jnp.arange(8, dtype=jnp.int32)
    mask_bits = jnp.bitwise_and(jnp.right_shift(packed[..., :, None, :], shifts[:, None]), 1)
    return mask_bits.reshape(packed.shape[:-2] + (packed.shape[-2] * 8, packed.shape[-1]))

def reference(queries, keys, values, block_ids, masks, gate_input, w_gate):
    score_scale = 1.0 / math.sqrt(F)
    highest = lax.Precision.HIGHEST

    def group(group_index):
        query_tiles = queries[group_index].reshape(QT, TILE, F).astype(jnp.float32)

        def team_step(totals, team_index):
            key_blocks = keys[:, team_index].reshape(N_BLK * KB, TILE, F)
            value_blocks = values[:, team_index].reshape(N_BLK * KB, TILE, F)
            block_list = block_ids[group_index, team_index]
            key_tiles = key_blocks[block_list].astype(jnp.float32)
            value_tiles = value_blocks[block_list].astype(jnp.float32)
            scores = jnp.einsum('qjbf,qaf->qjba', key_tiles, query_tiles, precision=highest) * score_scale
            mask_bits = unpack(masks[group_index, team_index]).astype(jnp.float32)
            weights = (mask_bits * jax.nn.sigmoid(scores)).astype(jnp.bfloat16)
            weights = lax.optimization_barrier(weights).astype(jnp.float32)
            added = jnp.einsum('qjba,qjbf->qaf', weights, value_tiles, precision=highest)
            return (totals + added, None)
        totals, _ = lax.scan(team_step, jnp.zeros((QT, TILE, F), jnp.float32), jnp.arange(N_TEAM, dtype=jnp.int32))
        aggregate = totals.reshape(QT * TILE, F)
        gate_pre = jnp.dot(gate_input[group_index], w_gate, preferred_element_type=jnp.float32)
        normed = aggregate * lax.rsqrt(lax.optimization_barrier(jnp.mean(aggregate * aggregate, axis=-1, keepdims=True)) + 1e-06)
        return (jax.nn.silu(gate_pre) * normed).astype(jnp.bfloat16)
    return lax.map(group, jnp.arange(N_BLK, dtype=jnp.int32))
```

```python
import functools
import math

import jax
import jax.numpy as jnp
from jax import lax
from jax.experimental import pallas as pl
from jax.experimental.pallas import tpu as pltpu
from jax.sharding import Mesh, PartitionSpec as P

CORES = 2
Y_SIZE = 4


def fetch(array, axis, size, distance):
    return lax.ppermute(array, axis, [(i, (i - distance) % size) for i in range(size)])


def tree_sum(parts):
    terms = [part.astype(jnp.float32) for part in parts]
    while len(terms) > 1:
        terms = [a + b for a, b in zip(terms[::2], terms[1::2])]
    return terms[0]


def attend_kernel(n_x, n_y, score_scale, ids_ref, *refs):
    pieces, refs = refs[: 2 * n_x], refs[2 * n_x :]
    query_pieces, refs = refs[:n_y], refs[n_y:]
    masks_ref, out_ref, kv, queries, kv_sem, q_sem = refs
    tiles, slots, words, tile_rows = masks_ref.shape
    x, core, y = lax.axis_index("x"), lax.axis_index("core"), lax.axis_index("y")
    y_tiles = tiles // n_y
    copies = []
    for d in range(n_y):
        first = lax.rem(y + d, n_y) * y_tiles
        copies.append(
            pltpu.make_async_copy(query_pieces[d], queries.at[pl.ds(first, y_tiles)], q_sem.at[d])
        )
    for d in range(n_x):
        for c in range(CORES):
            owner = lax.rem(x + d, n_x) * CORES + (core if c == 0 else 1 - core)
            at = d * CORES + c
            copies.append(pltpu.make_async_copy(pieces[at], kv.at[owner], kv_sem.at[at]))
    for copy in copies:
        copy.start()
    for copy in copies:
        copy.wait()
    shifts = lax.rem(lax.broadcasted_iota(jnp.int32, (tile_rows, tile_rows), 0), 8)

    def tile_step(tile, carry):
        ids = [ids_ref[tile, slot] for slot in range(slots)]
        owners = [lax.div(i, 2) for i in ids]
        halves = [lax.rem(i, 2) for i in ids]
        query = queries[tile]
        weights = []
        for slot in range(slots):
            scores = lax.dot_general(
                kv[owners[slot], halves[slot]],
                query,
                (((1,), (1,)), ((), ())),
                preferred_element_type=jnp.float32,
            )
            packed = masks_ref[tile, slot]
            packed = jnp.broadcast_to(packed[:, None, :], (words, 8, tile_rows))
            packed = packed.reshape(words * 8, tile_rows)
            bits = jnp.bitwise_and(jnp.right_shift(packed, shifts), 1)
            sigmoid = jax.nn.sigmoid(scores * score_scale)
            weights.append(jnp.where(bits == 1, sigmoid, 0.0).astype(jnp.bfloat16))
        weights = jnp.concatenate(weights, axis=0)
        value_rows = jnp.concatenate(
            [kv[owners[slot], 2 + halves[slot]] for slot in range(slots)], axis=0
        )
        added = lax.dot_general(
            weights, value_rows, (((0,), (0,)), ((), ())), preferred_element_type=jnp.float32
        )
        out_ref[tile] = added.astype(out_ref.dtype)
        return carry

    lax.fori_loop(0, tiles, tile_step, 0)


def attend(pieces, query_pieces, block_list, masks, n_x, n_y):
    tiles, slots, words, tile_rows = masks.shape
    width = query_pieces[0].shape[-1]
    pieces = [p.reshape(4, tile_rows, width) for p in pieces]
    query_pieces = [q.reshape(tiles // n_y, tile_rows, width) for q in query_pieces]
    vmem = pl.BlockSpec(memory_space=pltpu.VMEM)
    return pl.pallas_call(
        functools.partial(attend_kernel, n_x, n_y, 1.0 / math.sqrt(width)),
        out_shape=jax.ShapeDtypeStruct((tiles, tile_rows, width), jnp.bfloat16),
        in_specs=[pl.BlockSpec(memory_space=pltpu.SMEM)]
        + [vmem] * (len(pieces) + len(query_pieces) + 1),
        out_specs=vmem,
        scratch_shapes=[
            pltpu.VMEM((len(pieces), 4, tile_rows, width), jnp.bfloat16),
            pltpu.VMEM((tiles, tile_rows, width), jnp.bfloat16),
            pltpu.SemaphoreType.DMA((len(pieces),)),
            pltpu.SemaphoreType.DMA((n_y,)),
        ],
        cost_estimate=pl.CostEstimate(
            flops=4 * tiles * slots * tile_rows * tile_rows * width,
            bytes_accessed=8 << 20,
            transcendentals=tiles * slots * tile_rows * tile_rows,
        ),
    )(block_list, *pieces, *query_pieces, masks)


def per_device(n_x, n_y, n_z, queries, keys, values, block_ids, masks, gate_input, w_gate):
    block_list = block_ids[0, 0]
    mask_words = masks[0, 0]
    local_rows, width = queries.shape[1:]
    own = jnp.concatenate([keys[0, 0], values[0, 0]], axis=0)
    along_x = [fetch(own, "x", n_x, d) for d in range(1, n_x)]
    own_swapped = fetch(own, "core", CORES, 1)
    column = lax.all_gather(queries[0], "z", axis=0, tiled=True)
    along_x, column = lax.optimization_barrier((along_x, column))
    query_pieces = [column] + [fetch(column, "y", n_y, d) for d in range(1, n_y)]
    swapped = [own_swapped] + [fetch(piece, "core", CORES, 1) for piece in along_x]
    pieces = [p for pair in zip([own] + along_x, swapped) for p in pair]
    added = attend(pieces, query_pieces, block_list, mask_words, n_x, n_y)
    parts = lax.all_to_all(added.reshape(n_y, n_z * local_rows, width), "y", 0, 0)
    summed = tree_sum(parts).astype(jnp.bfloat16)
    parts = lax.all_to_all(summed.reshape(n_z, local_rows, width), "z", 0, 0)
    aggregate = tree_sum(parts)
    gate_pre = jnp.dot(gate_input[0], w_gate, preferred_element_type=jnp.float32)
    normed = aggregate * lax.rsqrt(jnp.mean(aggregate * aggregate, axis=-1, keepdims=True) + 1e-06)
    return (jax.nn.silu(gate_pre) * normed).astype(jnp.bfloat16)[None]


def solution(mesh):
    n_x, n_y = mesh.shape["blk"] // CORES, Y_SIZE
    n_z = mesh.shape["team"] // n_y
    fine = Mesh(mesh.devices.reshape(n_x, CORES, n_y, n_z), ("x", "core", "y", "z"))
    blk, team = ("x", "core"), ("y", "z")
    return jax.shard_map(
        functools.partial(per_device, n_x, n_y, n_z),
        mesh=fine,
        in_specs=(
            P(blk, team, None),
            P(blk, team, None, None),
            P(blk, team, None, None),
            P(blk, team, None, None),
            P(blk, team, None, None, None, None),
            P(blk, team, None),
            P(),
        ),
        out_specs=P(blk, team, None),
        check_vma=False,
    )
```

```python
import functools
import math

import jax
import jax.numpy as jnp
from jax import lax
from jax.experimental import pallas as pl
from jax.experimental.pallas import tpu as pltpu
from jax.sharding import Mesh, PartitionSpec as P

CORES = 2
Y_SIZE = 4
VMEM_LIMIT = 24 << 20
VMEM_SPEC = pl.BlockSpec(memory_space=pltpu.VMEM)


def fetch(array, axis, size, distance):
    return lax.ppermute(array, axis, [(i, (i - distance) % size) for i in range(size)])


def tree_sum(parts):
    terms = [part.astype(jnp.float32) for part in parts]
    while len(terms) > 1:
        terms = [a + b for a, b in zip(terms[::2], terms[1::2])]
    return terms[0]


def pack_kernel(*refs):
    out_ref = refs[-1]
    for at, ref in enumerate(refs[:-1]):
        out_ref[at] = ref[...]


def pack(*arrays):
    return pl.pallas_call(
        pack_kernel,
        out_shape=jax.ShapeDtypeStruct((len(arrays), *arrays[0].shape), arrays[0].dtype),
        in_specs=[VMEM_SPEC] * len(arrays),
        out_specs=VMEM_SPEC,
        compiler_params=pltpu.CompilerParams(vmem_limit_bytes=VMEM_LIMIT),
    )(*arrays)


def attend_tile(kv, query, ids, packed_ref, tile, score_scale):
    slots, words, tile_rows = packed_ref.shape[1:]
    shifts = lax.rem(lax.broadcasted_iota(jnp.int32, (tile_rows, tile_rows), 0), 8)
    weights = []
    for slot in range(slots):
        scores = lax.dot_general(
            kv[lax.div(ids[slot], 2), lax.rem(ids[slot], 2)],
            query,
            (((1,), (1,)), ((), ())),
            preferred_element_type=jnp.float32,
        )
        packed = packed_ref[tile, slot]
        packed = jnp.broadcast_to(packed[:, None, :], (words, 8, tile_rows))
        packed = packed.reshape(words * 8, tile_rows)
        bits = jnp.bitwise_and(jnp.right_shift(packed, shifts), 1)
        sigmoid = jax.nn.sigmoid(scores * score_scale)
        weights.append(jnp.where(bits == 1, sigmoid, 0.0).astype(jnp.bfloat16))
    weights = jnp.concatenate(weights, axis=0)
    value_rows = jnp.concatenate(
        [kv[lax.div(ids[slot], 2), 2 + lax.rem(ids[slot], 2)] for slot in range(slots)], axis=0
    )
    return lax.dot_general(
        weights, value_rows, (((0,), (0,)), ((), ())), preferred_element_type=jnp.float32
    )


def attend_column(d, n_y, score_scale, ids_ref, kv, query_ref, masks_ref, out_ref):
    slots = masks_ref.shape[1]
    y_tiles = out_ref.shape[0]
    first = lax.rem(lax.axis_index("y") + d, n_y) * y_tiles
    for i in range(y_tiles):
        ids = [ids_ref[first + i, slot] for slot in range(slots)]
        added = attend_tile(kv, query_ref[i], ids, masks_ref, first + i, score_scale)
        out_ref[i] = added.astype(out_ref.dtype)


def assemble(n_x, mine, swapped, kv):
    x, core = lax.axis_index("x"), lax.axis_index("core")
    for piece in range(n_x):
        base = lax.rem(x + piece, n_x) * CORES
        kv[base + core] = mine[piece][...]
        kv[base + 1 - core] = swapped[piece]


def first_kernel(d, n_x, n_y, score_scale, ids_ref, *refs):
    mine, (swapped, query_ref, masks_ref, kv, out_ref) = refs[:n_x], refs[n_x:]
    assemble(n_x, mine, swapped, kv)
    attend_column(d, n_y, score_scale, ids_ref, kv, query_ref, masks_ref, out_ref)


def attend_cost(tiles, slots, tile_rows, width):
    return pl.CostEstimate(
        flops=4 * tiles * slots * tile_rows * tile_rows * width,
        bytes_accessed=4 << 20,
        transcendentals=tiles * slots * tile_rows * tile_rows,
    )


def attend_first(d, block_list, mine, swapped, query, masks, n_x, n_y):
    tiles, slots, _, tile_rows = masks.shape
    width = query.shape[-1]
    y_tiles = tiles // n_y
    kv_shape = (4, tile_rows, width)
    kv, added = pl.pallas_call(
        functools.partial(first_kernel, d, n_x, n_y, 1.0 / math.sqrt(width)),
        out_shape=(
            jax.ShapeDtypeStruct((n_x * CORES, *kv_shape), jnp.bfloat16),
            jax.ShapeDtypeStruct((y_tiles, tile_rows, width), jnp.bfloat16),
        ),
        in_specs=[pl.BlockSpec(memory_space=pltpu.SMEM)] + [VMEM_SPEC] * (n_x + 3),
        out_specs=(VMEM_SPEC, VMEM_SPEC),
        compiler_params=pltpu.CompilerParams(vmem_limit_bytes=VMEM_LIMIT),
        cost_estimate=attend_cost(y_tiles, slots, tile_rows, width),
    )(
        block_list,
        *[piece.reshape(kv_shape) for piece in mine],
        swapped.reshape(n_x, *kv_shape),
        query.reshape(-1, tile_rows, width),
        masks,
    )
    return kv, added.reshape(-1, width)


def attend_next(d, block_list, kv, query, masks, n_y, dtype=jnp.bfloat16):
    tiles, slots, _, tile_rows = masks.shape
    width = query.shape[-1]
    y_tiles = tiles // n_y
    return pl.pallas_call(
        functools.partial(attend_column, d, n_y, 1.0 / math.sqrt(width)),
        out_shape=jax.ShapeDtypeStruct((y_tiles, tile_rows, width), dtype),
        in_specs=[pl.BlockSpec(memory_space=pltpu.SMEM)] + [VMEM_SPEC] * 3,
        out_specs=VMEM_SPEC,
        compiler_params=pltpu.CompilerParams(vmem_limit_bytes=VMEM_LIMIT),
        cost_estimate=attend_cost(y_tiles, slots, tile_rows, width),
    )(block_list, kv, query.reshape(-1, tile_rows, width), masks).reshape(-1, width)


def per_device(n_x, n_y, n_z, queries, keys, values, block_ids, masks, gate_input, w_gate):
    block_list = block_ids[0, 0]
    mask_words = masks[0, 0]
    local_rows, width = queries.shape[1:]
    query = queries[0]
    own = jnp.concatenate([keys[0, 0], values[0, 0]], axis=0)
    along_x = []
    for d in range(1, n_x):
        along_x.append(fetch(own, "x", n_x, d))
    column = lax.all_to_all(jnp.broadcast_to(query, (n_z, *query.shape)), "z", 0, 0)
    column = column.reshape(n_z * local_rows, width)
    along_x, column = lax.optimization_barrier((along_x, column))
    mine = [own, *along_x]
    packed = pack(*mine)
    swapped = fetch(packed, "core", CORES, 1)
    columns = [column]
    for d in range(1, n_y):
        columns.append(fetch(column, "y", n_y, d))
    kv, parts = None, []
    for d in (1, 3, 2, 0):
        if kv is None:
            kv, added = attend_first(d, block_list, mine, swapped, columns[d], mask_words, n_x, n_y)
        else:
            dtype = jnp.bfloat16 if d else jnp.float32
            added = attend_next(d, block_list, kv, columns[d], mask_words, n_y, dtype)
        parts.append(fetch(added, "y", n_y, -d) if d else added)
    summed = tree_sum(parts).astype(jnp.bfloat16)
    parts = lax.all_to_all(summed.reshape(n_z, local_rows, width), "z", 0, 0)
    aggregate = tree_sum(parts)
    gate_pre = jnp.dot(gate_input[0], w_gate, preferred_element_type=jnp.float32)
    normed = aggregate * lax.rsqrt(jnp.mean(aggregate * aggregate, axis=-1, keepdims=True) + 1e-06)
    return (jax.nn.silu(gate_pre) * normed).astype(jnp.bfloat16)[None]


def solution(mesh):
    n_x, n_y = mesh.shape["blk"] // CORES, Y_SIZE
    n_z = mesh.shape["team"] // n_y
    fine = Mesh(mesh.devices.reshape(n_x, CORES, n_y, n_z), ("x", "core", "y", "z"))
    blk, team = ("x", "core"), ("y", "z")

    def program(*args):
        return per_device(n_x, n_y, n_z, *args)

    return jax.shard_map(
        program,
        mesh=fine,
        in_specs=(
            P(blk, team, None),
            P(blk, team, None, None),
            P(blk, team, None, None),
            P(blk, team, None, None),
            P(blk, team, None, None, None, None),
            P(blk, team, None),
            P(),
        ),
        out_specs=P(blk, team, None),
        check_vma=False,
    )
```

```python
import functools
import math

import jax
import jax.numpy as jnp
from jax import lax
from jax.experimental import pallas as pl
from jax.experimental.pallas import tpu as pltpu
from jax.sharding import Mesh, PartitionSpec as P

CORES = 2
Y_SIZE = 4
VMEM_LIMIT = 24 << 20
VMEM_SPEC = pl.BlockSpec(memory_space=pltpu.VMEM)


def fetch(array, axis, size, distance):
    return lax.ppermute(array, axis, [(i, (i - distance) % size) for i in range(size)])


def tree_sum(parts):
    terms = [part.astype(jnp.float32) for part in parts]
    while len(terms) > 1:
        terms = [a + b for a, b in zip(terms[::2], terms[1::2])]
    return terms[0]


def pack_kernel(*refs):
    out_ref = refs[-1]
    for at, ref in enumerate(refs[:-1]):
        out_ref[at] = ref[...]


def pack(*arrays):
    return pl.pallas_call(
        pack_kernel,
        out_shape=jax.ShapeDtypeStruct((len(arrays), *arrays[0].shape), arrays[0].dtype),
        in_specs=[VMEM_SPEC] * len(arrays),
        out_specs=VMEM_SPEC,
        compiler_params=pltpu.CompilerParams(vmem_limit_bytes=VMEM_LIMIT),
    )(*arrays)


def attend_tile(kv, query, ids, packed_ref, tile, score_scale):
    slots, words, tile_rows = packed_ref.shape[1:]
    shifts = lax.rem(lax.broadcasted_iota(jnp.int32, (tile_rows, tile_rows), 0), 8)
    weights = []
    for slot in range(slots):
        scores = lax.dot_general(
            kv[lax.div(ids[slot], 2), lax.rem(ids[slot], 2)],
            query,
            (((1,), (1,)), ((), ())),
            preferred_element_type=jnp.float32,
        )
        packed = packed_ref[tile, slot]
        packed = jnp.broadcast_to(packed[:, None, :], (words, 8, tile_rows))
        packed = packed.reshape(words * 8, tile_rows)
        bits = jnp.bitwise_and(jnp.right_shift(packed, shifts), 1)
        sigmoid = jax.nn.sigmoid(scores * score_scale)
        weights.append(jnp.where(bits == 1, sigmoid, 0.0).astype(jnp.bfloat16))
    weights = jnp.concatenate(weights, axis=0)
    value_rows = jnp.concatenate(
        [kv[lax.div(ids[slot], 2), 2 + lax.rem(ids[slot], 2)] for slot in range(slots)], axis=0
    )
    return lax.dot_general(
        weights, value_rows, (((0,), (0,)), ((), ())), preferred_element_type=jnp.float32
    )


def attend_column(d, n_y, score_scale, ids_ref, kv, query_ref, masks_ref, out_ref):
    slots = masks_ref.shape[1]
    y_tiles = out_ref.shape[0]
    first = lax.rem(lax.axis_index("y") + d, n_y) * y_tiles
    for i in range(y_tiles):
        ids = [ids_ref[first + i, slot] for slot in range(slots)]
        added = attend_tile(kv, query_ref[i], ids, masks_ref, first + i, score_scale)
        out_ref[i] = added.astype(out_ref.dtype)


def assemble(n_x, mine, swapped, kv):
    x, core = lax.axis_index("x"), lax.axis_index("core")
    for piece in range(n_x):
        base = lax.rem(x + piece, n_x) * CORES
        kv[base + core] = mine[piece][...]
        kv[base + 1 - core] = swapped[piece]


def first_kernel(d, n_x, n_y, score_scale, ids_ref, *refs):
    mine, (swapped, query_ref, masks_ref, kv, out_ref) = refs[:n_x], refs[n_x:]
    assemble(n_x, mine, swapped, kv)
    attend_column(d, n_y, score_scale, ids_ref, kv, query_ref, masks_ref, out_ref)


def attend_cost(tiles, slots, tile_rows, width):
    return pl.CostEstimate(
        flops=4 * tiles * slots * tile_rows * tile_rows * width,
        bytes_accessed=4 << 20,
        transcendentals=tiles * slots * tile_rows * tile_rows,
    )


def attend_first(d, block_list, mine, swapped, query, masks, n_x, n_y):
    tiles, slots, _, tile_rows = masks.shape
    width = query.shape[-1]
    y_tiles = tiles // n_y
    kv_shape = (4, tile_rows, width)
    kv, added = pl.pallas_call(
        functools.partial(first_kernel, d, n_x, n_y, 1.0 / math.sqrt(width)),
        out_shape=(
            jax.ShapeDtypeStruct((n_x * CORES, *kv_shape), jnp.bfloat16),
            jax.ShapeDtypeStruct((y_tiles, tile_rows, width), jnp.bfloat16),
        ),
        in_specs=[pl.BlockSpec(memory_space=pltpu.SMEM)] + [VMEM_SPEC] * (n_x + 3),
        out_specs=(VMEM_SPEC, VMEM_SPEC),
        compiler_params=pltpu.CompilerParams(vmem_limit_bytes=VMEM_LIMIT),
        cost_estimate=attend_cost(y_tiles, slots, tile_rows, width),
    )(
        block_list,
        *[piece.reshape(kv_shape) for piece in mine],
        swapped.reshape(n_x, *kv_shape),
        query.reshape(-1, tile_rows, width),
        masks,
    )
    return kv, added.reshape(-1, width)


def attend_next(d, block_list, kv, query, masks, n_y, dtype=jnp.bfloat16):
    tiles, slots, _, tile_rows = masks.shape
    width = query.shape[-1]
    y_tiles = tiles // n_y
    return pl.pallas_call(
        functools.partial(attend_column, d, n_y, 1.0 / math.sqrt(width)),
        out_shape=jax.ShapeDtypeStruct((y_tiles, tile_rows, width), dtype),
        in_specs=[pl.BlockSpec(memory_space=pltpu.SMEM)] + [VMEM_SPEC] * 3,
        out_specs=VMEM_SPEC,
        compiler_params=pltpu.CompilerParams(vmem_limit_bytes=VMEM_LIMIT),
        cost_estimate=attend_cost(y_tiles, slots, tile_rows, width),
    )(block_list, kv, query.reshape(-1, tile_rows, width), masks).reshape(-1, width)


def per_device(n_x, n_y, n_z, queries, keys, values, block_ids, masks, gate_input, w_gate):
    block_list = block_ids[0, 0]
    mask_words = masks[0, 0]
    local_rows, width = queries.shape[1:]
    query = queries[0]
    own = jnp.concatenate([keys[0, 0], values[0, 0]], axis=0)
    along_x = []
    for d in range(1, n_x):
        along_x.append(fetch(own, "x", n_x, d))
    column = lax.all_to_all(jnp.broadcast_to(query, (n_z, *query.shape)), "z", 0, 0)
    column = column.reshape(n_z * local_rows, width)
    along_x, column = lax.optimization_barrier((along_x, column))
    mine = [own, *along_x]
    packed = pack(*mine)
    swapped = fetch(packed, "core", CORES, 1)
    columns = {0: column}
    for d in (1, n_y - 1):
        columns[d] = fetch(column, "y", n_y, d)
    columns[2] = fetch(column, "y", n_y, 2)
    kv, parts = None, []
    for d in (2, 3, 1, 0):
        if kv is None:
            kv, added = attend_first(d, block_list, mine, swapped, columns[d], mask_words, n_x, n_y)
        else:
            dtype = jnp.bfloat16 if d else jnp.float32
            added = attend_next(d, block_list, kv, columns[d], mask_words, n_y, dtype)
        parts.append(fetch(added, "y", n_y, -d) if d else added)
    summed = tree_sum(parts).astype(jnp.bfloat16)
    parts = lax.all_to_all(summed.reshape(n_z, local_rows, width), "z", 0, 0)
    aggregate = tree_sum(parts)
    gate_pre = jnp.dot(gate_input[0], w_gate, preferred_element_type=jnp.float32)
    normed = aggregate * lax.rsqrt(jnp.mean(aggregate * aggregate, axis=-1, keepdims=True) + 1e-06)
    return (jax.nn.silu(gate_pre) * normed).astype(jnp.bfloat16)[None]


def solution(mesh):
    n_x, n_y = mesh.shape["blk"] // CORES, Y_SIZE
    n_z = mesh.shape["team"] // n_y
    fine = Mesh(mesh.devices.reshape(n_x, CORES, n_y, n_z), ("x", "core", "y", "z"))
    blk, team = ("x", "core"), ("y", "z")

    def program(*args):
        return per_device(n_x, n_y, n_z, *args)

    return jax.shard_map(
        program,
        mesh=fine,
        in_specs=(
            P(blk, team, None),
            P(blk, team, None, None),
            P(blk, team, None, None),
            P(blk, team, None, None),
            P(blk, team, None, None, None, None),
            P(blk, team, None),
            P(),
        ),
        out_specs=P(blk, team, None),
        check_vma=False,
    )
```

```python
import functools
import math

import jax
import jax.numpy as jnp
from jax import lax
from jax.experimental import pallas as pl
from jax.experimental.pallas import tpu as pltpu
from jax.sharding import Mesh, PartitionSpec as P

CORES = 2
Y_SIZE = 4
VMEM_LIMIT = 24 << 20
VMEM_SPEC = pl.BlockSpec(memory_space=pltpu.VMEM)


def fetch(array, axis, size, distance):
    return lax.ppermute(array, axis, [(i, (i - distance) % size) for i in range(size)])


def tree_sum(parts):
    terms = [part.astype(jnp.float32) for part in parts]
    while len(terms) > 1:
        terms = [a + b for a, b in zip(terms[::2], terms[1::2])]
    return terms[0]


def pack_kernel(*refs):
    out_ref = refs[-1]
    for at, ref in enumerate(refs[:-1]):
        out_ref[at] = ref[...]


def pack(*arrays):
    return pl.pallas_call(
        pack_kernel,
        out_shape=jax.ShapeDtypeStruct((len(arrays), *arrays[0].shape), arrays[0].dtype),
        in_specs=[VMEM_SPEC] * len(arrays),
        out_specs=VMEM_SPEC,
        compiler_params=pltpu.CompilerParams(vmem_limit_bytes=VMEM_LIMIT),
    )(*arrays)


def gate_kernel(gate_ref, w_ref, out_ref):
    gate_pre = jnp.dot(gate_ref[...], w_ref[...], preferred_element_type=jnp.float32)
    out_ref[...] = jax.nn.silu(gate_pre)


def gate(gate_input, w_gate):
    return pl.pallas_call(
        gate_kernel,
        out_shape=jax.ShapeDtypeStruct(gate_input.shape, jnp.float32),
        in_specs=[VMEM_SPEC] * 2,
        out_specs=VMEM_SPEC,
        compiler_params=pltpu.CompilerParams(vmem_limit_bytes=VMEM_LIMIT),
    )(gate_input, w_gate)


def attend_tile(kv, query, ids, packed_ref, tile, score_scale):
    slots, words, tile_rows = packed_ref.shape[1:]
    shifts = lax.rem(lax.broadcasted_iota(jnp.int32, (tile_rows, tile_rows), 0), 8)
    weights = []
    for slot in range(slots):
        scores = lax.dot_general(
            kv[lax.div(ids[slot], 2), lax.rem(ids[slot], 2)],
            query,
            (((1,), (1,)), ((), ())),
            preferred_element_type=jnp.float32,
        )
        packed = packed_ref[tile, slot]
        packed = jnp.broadcast_to(packed[:, None, :], (words, 8, tile_rows))
        packed = packed.reshape(words * 8, tile_rows)
        bits = jnp.bitwise_and(jnp.right_shift(packed, shifts), 1)
        sigmoid = jax.nn.sigmoid(scores * score_scale)
        weights.append(jnp.where(bits == 1, sigmoid, 0.0).astype(jnp.bfloat16))
    weights = jnp.concatenate(weights, axis=0)
    value_rows = jnp.concatenate(
        [kv[lax.div(ids[slot], 2), 2 + lax.rem(ids[slot], 2)] for slot in range(slots)], axis=0
    )
    return lax.dot_general(
        weights, value_rows, (((0,), (0,)), ((), ())), preferred_element_type=jnp.float32
    )


def attend_column(d, n_y, score_scale, ids_ref, kv, query_ref, masks_ref, out_ref):
    slots = masks_ref.shape[1]
    y_tiles = out_ref.shape[0]
    first = lax.rem(lax.axis_index("y") + d, n_y) * y_tiles
    for i in range(y_tiles):
        ids = [ids_ref[first + i, slot] for slot in range(slots)]
        added = attend_tile(kv, query_ref[i], ids, masks_ref, first + i, score_scale)
        out_ref[i] = added.astype(out_ref.dtype)


def assemble(n_x, mine, swapped, kv):
    x, core = lax.axis_index("x"), lax.axis_index("core")
    for piece in range(n_x):
        base = lax.rem(x + piece, n_x) * CORES
        kv[base + core] = mine[piece][...]
        kv[base + 1 - core] = swapped[piece]


def first_kernel(d, n_x, n_y, score_scale, ids_ref, *refs):
    mine, (swapped, query_ref, masks_ref, kv, out_ref) = refs[:n_x], refs[n_x:]
    assemble(n_x, mine, swapped, kv)
    attend_column(d, n_y, score_scale, ids_ref, kv, query_ref, masks_ref, out_ref)


def attend_cost(tiles, slots, tile_rows, width):
    return pl.CostEstimate(
        flops=4 * tiles * slots * tile_rows * tile_rows * width,
        bytes_accessed=4 << 20,
        transcendentals=tiles * slots * tile_rows * tile_rows,
    )


def attend_first(d, block_list, mine, swapped, query, masks, n_x, n_y):
    tiles, slots, _, tile_rows = masks.shape
    width = query.shape[-1]
    y_tiles = tiles // n_y
    kv_shape = (4, tile_rows, width)
    kv, added = pl.pallas_call(
        functools.partial(first_kernel, d, n_x, n_y, 1.0 / math.sqrt(width)),
        out_shape=(
            jax.ShapeDtypeStruct((n_x * CORES, *kv_shape), jnp.bfloat16),
            jax.ShapeDtypeStruct((y_tiles, tile_rows, width), jnp.bfloat16),
        ),
        in_specs=[pl.BlockSpec(memory_space=pltpu.SMEM)] + [VMEM_SPEC] * (n_x + 3),
        out_specs=(VMEM_SPEC, VMEM_SPEC),
        compiler_params=pltpu.CompilerParams(vmem_limit_bytes=VMEM_LIMIT),
        cost_estimate=attend_cost(y_tiles, slots, tile_rows, width),
    )(
        block_list,
        *[piece.reshape(kv_shape) for piece in mine],
        swapped.reshape(n_x, *kv_shape),
        query.reshape(-1, tile_rows, width),
        masks,
    )
    return kv, added.reshape(-1, width)


def attend_next(d, block_list, kv, query, masks, n_y, dtype=jnp.bfloat16):
    tiles, slots, _, tile_rows = masks.shape
    width = query.shape[-1]
    y_tiles = tiles // n_y
    return pl.pallas_call(
        functools.partial(attend_column, d, n_y, 1.0 / math.sqrt(width)),
        out_shape=jax.ShapeDtypeStruct((y_tiles, tile_rows, width), dtype),
        in_specs=[pl.BlockSpec(memory_space=pltpu.SMEM)] + [VMEM_SPEC] * 3,
        out_specs=VMEM_SPEC,
        compiler_params=pltpu.CompilerParams(vmem_limit_bytes=VMEM_LIMIT),
        cost_estimate=attend_cost(y_tiles, slots, tile_rows, width),
    )(block_list, kv, query.reshape(-1, tile_rows, width), masks).reshape(-1, width)


def per_device(n_x, n_y, n_z, queries, keys, values, block_ids, masks, gate_input, w_gate):
    block_list = block_ids[0, 0]
    mask_words = masks[0, 0]
    local_rows, width = queries.shape[1:]
    query = queries[0]
    own = jnp.concatenate([keys[0, 0], values[0, 0]], axis=0)
    along_x = []
    for d in range(1, n_x):
        along_x.append(fetch(own, "x", n_x, d))
    column = lax.all_to_all(jnp.broadcast_to(query, (n_z, *query.shape)), "z", 0, 0)
    column = column.reshape(n_z * local_rows, width)
    along_x, column = lax.optimization_barrier((along_x, column))
    mine = [own, *along_x]
    packed = pack(*mine)
    swapped = fetch(packed, "core", CORES, 1)
    columns = {0: column}
    for d in (1, n_y - 1):
        columns[d] = fetch(column, "y", n_y, d)
    columns[2] = fetch(column, "y", n_y, 2)
    kv, parts = None, []
    for d in (2, 1, 3, 0):
        if kv is None:
            kv, added = attend_first(d, block_list, mine, swapped, columns[d], mask_words, n_x, n_y)
        else:
            dtype = jnp.bfloat16 if d else jnp.float32
            added = attend_next(d, block_list, kv, columns[d], mask_words, n_y, dtype)
        parts.append(fetch(added, "y", n_y, -d) if d else added)
    summed = tree_sum(parts).astype(jnp.bfloat16)
    parts = lax.all_to_all(summed.reshape(n_z, local_rows, width), "z", 0, 0)
    aggregate = tree_sum(parts)
    gated = gate(gate_input[0], w_gate)
    normed = aggregate * lax.rsqrt(jnp.mean(aggregate * aggregate, axis=-1, keepdims=True) + 1e-06)
    return (gated * normed).astype(jnp.bfloat16)[None]


def solution(mesh):
    n_x, n_y = mesh.shape["blk"] // CORES, Y_SIZE
    n_z = mesh.shape["team"] // n_y
    fine = Mesh(mesh.devices.reshape(n_x, CORES, n_y, n_z), ("x", "core", "y", "z"))
    blk, team = ("x", "core"), ("y", "z")

    def program(*args):
        return per_device(n_x, n_y, n_z, *args)

    return jax.shard_map(
        program,
        mesh=fine,
        in_specs=(
            P(blk, team, None),
            P(blk, team, None, None),
            P(blk, team, None, None),
            P(blk, team, None, None),
            P(blk, team, None, None, None, None),
            P(blk, team, None),
            P(),
        ),
        out_specs=P(blk, team, None),
        check_vma=False,
    )
```
